32 devices in a mesh: row: 2 (over core), col: 4 (over z), kk: 4 (over y, x).
Axes of the slice: x: 2, y: 2, z: 4, core: 2. Of those that a mesh axis runs over, the one named last changes fastest.
Arguments:
- contribution: float32 [32, 256, 16, 512], P('kk', 'row', None, 'col'), may hold values from -6 to 6
- left_panel: float32 [32, 256, 4, 768], P(None, 'row', 'kk', 'col'), may hold values from -6 to 6
- right_panel: float32 [4, 768, 16, 512], P('kk', 'row', None, 'col'), may hold values from -0.109375 to 0.109375
Outputs:
- updated: float32 [32, 256, 16, 512], P('kk', 'row', None, 'col')
The draws below stay inside these ranges and needn't reach their ends.
All inputs are finite; a program needn't handle non-finite values.
Results may differ from the reference program's by a relative error of at most 0.00005.
Values sent between devices are 32-bit elements; how exact they have to be, the bound alone decides.
No kernel may reach another device: no remote copies, remote signals or barrier semaphores. Data moves between devices by JAX's collectives and lax.ppermute only.
A program may use at most 128 MiB of HBM per device.

```python
import jax
import jax.numpy as jnp
from jax import lax

N = 8192
K = 3072
BS = 128
RL = 32
CL = 16
KQ = 768
N_ROW = 2
N_COL = 4
N_KK = 4


def shard_levels(stream_key, shape, shards, least, high):
    def one(dim, shards_of):
        steps = jax.random.uniform(jax.random.fold_in(jax.random.fold_in(stream_key, 6), dim), (shards_of,), jnp.float32, least / len(shards), high / len(shards))
        return jnp.repeat(jnp.exp(steps), shape[dim] // shards_of).reshape((-1,) + (1,) * (len(shape) - dim - 1))

    factor_of = one(*shards[0])
    for cut in shards[1:]:
        factor_of = factor_of * one(*cut)
    return factor_of


def normal_values(own_key, dims, scale, reach, shards=(), held_as=jnp.bfloat16):
    array = jax.random.normal(own_key, dims, jnp.float32) * scale
    if len(shards) > 0:
        array = shard_levels(own_key, dims, shards, -0.22, 0.18) * array
    return jnp.clip(array, min=-reach, max=reach).astype(held_as)


def setup_inputs(seed: int = 0) -> dict:
    key_of = jax.random.split(jax.random.key(seed), 4)
    contribution = normal_values(key_of[0], (RL, N_ROW * BS, CL, N_COL * BS), 1.0, 6.0, ((0, 4), (1, 2), (3, 4)), jnp.float32)
    left_panel = normal_values(key_of[1], (RL, N_ROW * BS, N_KK, KQ), 1.0, 6.0, ((1, 2), (2, 4), (3, 4)), jnp.float32)
    right_panel = normal_values(key_of[2], (N_KK, KQ, CL, N_COL * BS), K ** -0.5, 0.109375, ((0, 4), (1, 2), (3, 4)), jnp.float32)
    return {"contribution": contribution, "left_panel": left_panel, "right_panel": right_panel}


def reference(contribution, left_panel, right_panel):
    left_matrix = left_panel.reshape(N, K)
    right_matrix = right_panel.reshape(K, N)
    product = jnp.dot(left_matrix, right_matrix, precision=lax.Precision.HIGHEST, preferred_element_type=jnp.float32)
    return contribution - product.reshape(contribution.shape)
```

```python
import functools

import jax
import jax.numpy as jnp
from jax import lax
from jax.experimental import pallas as pl
from jax.experimental.pallas import tpu as pltpu
from jax.sharding import PartitionSpec as P


LANES = 128
VMEM_LIMIT = 16 * 1024 * 1024


def split(value):
    high = value.astype(jnp.bfloat16)
    return high, (value - high.astype(jnp.float32)).astype(jnp.bfloat16)


def product(left_high, left_low, right_high, right_low):
    dot = functools.partial(jnp.dot, preferred_element_type=jnp.float32)
    return dot(left_high, right_high) + (dot(left_high, right_low) + dot(left_low, right_high))


def fetch(slot, flag, first, buffer, sem):
    count = buffer.shape[0]
    copies = []
    for ref, skip in zip(slot, first):
        copies.append(pltpu.make_async_copy(ref.at[pl.ds(skip, count)], buffer, sem))
    if len(copies) == 1:
        copies[0].start()
    else:
        pl.when(flag != 0)(copies[0].start)
        pl.when(flag == 0)(copies[1].start)
    return copies[0]


def add_kernel(counts, pieces, keep, scalars, acc_ref, *refs):
    right, refs = refs[:pieces], refs[pieces:]
    slots = []
    for count in counts:
        slots.append(refs[:count])
        refs = refs[count:]
    out_ref, right_high, right_low, buffers, sems, turned, left_high, left_low = refs
    width, rows = slots[0][0].shape[1:]
    row_blocks = buffers.shape[1]
    cut = right[0].shape[1]
    step = pl.program_id(0)
    lanes = pl.ds(pl.multiple_of(step * cut, cut), cut)
    mine = lanes if keep else slice(None)

    def copies(start):
        for index, slot in enumerate(slots):
            if start:
                fetch(slot, scalars[2 * index + 1], (0, 0), buffers.at[index], sems.at[index])
            else:
                pltpu.make_async_copy(slot[0].at[pl.ds(0, row_blocks)], buffers.at[index], sems.at[index]).wait()

    @pl.when(step == 0)
    def _():
        copies(True)
        turned[...] = jnp.zeros_like(turned)

    at = 0
    for piece in right:
        high, low = split(piece[...])
        right_high[at : at + piece.shape[0], mine] = high
        right_low[at : at + piece.shape[0], mine] = low
        at += piece.shape[0]

    @pl.when(step == 0)
    def _():
        copies(False)

        def one(block, carry):
            for index in range(len(slots)):
                at = pl.multiple_of(scalars[2 * index] * width, width)
                turned[pl.ds(at, width), :] = buffers[index, block]
            high, low = split(turned[...].T)
            at = pl.multiple_of(block * rows, rows)
            left_high[pl.ds(at, rows), :] = high
            left_low[pl.ds(at, rows), :] = low
            return carry

        lax.fori_loop(0, row_blocks, one, 0)

    out_ref[:, lanes] = acc_ref[:, lanes] - product(
        left_high[...], left_low[...], right_high[:, mine], right_low[:, mine]
    )


def add(acc, slots, scalars, right, keep):
    rows, cols = acc.shape
    depth = sum(piece.shape[0] for piece in right)
    flat = [array for slot in slots for array in slot]
    cut = min(cols, 2 * LANES)
    resident = pl.BlockSpec(memory_space=pltpu.VMEM)
    used = len(slots) * flat[0].shape[1]
    shape = jax.ShapeDtypeStruct((depth, cols), jnp.bfloat16)
    terms = [pltpu.VMEM((depth, cut), jnp.bfloat16)] * 2
    return pl.pallas_call(
        functools.partial(add_kernel, [len(slot) for slot in slots], len(right), keep),
        out_shape=[jax.ShapeDtypeStruct(acc.shape, acc.dtype)] + [shape, shape] * keep,
        grid_spec=pltpu.PrefetchScalarGridSpec(
            num_scalar_prefetch=1,
            grid=(cols // cut,),
            in_specs=[resident]
            + [pl.BlockSpec((piece.shape[0], cut), lambda i, s: (0, i)) for piece in right]
            + [pl.BlockSpec(memory_space=pl.ANY)] * len(flat),
            out_specs=[resident] + [resident] * (2 * keep),
            scratch_shapes=terms * (not keep)
            + [
                pltpu.VMEM((len(slots),) + flat[0].shape, jnp.float32),
                pltpu.SemaphoreType.DMA((len(slots),)),
                pltpu.VMEM((depth, flat[0].shape[2]), jnp.float32),
                pltpu.VMEM((rows, depth), jnp.bfloat16),
                pltpu.VMEM((rows, depth), jnp.bfloat16),
            ],
        ),
        input_output_aliases={1: 0},
        compiler_params=pltpu.CompilerParams(vmem_limit_bytes=VMEM_LIMIT),
        cost_estimate=pl.CostEstimate(
            flops=6 * rows * used * cols, bytes_accessed=4 * depth * cols, transcendentals=0
        ),
        name="add",
    )(scalars, acc, *right, *flat)


def fold_kernel(blocks, x_ref, acc_ref):
    rows = x_ref.shape[0] // blocks
    mine = pl.ds(pl.multiple_of(pl.program_id(0) * rows, rows), rows)
    for block in range(blocks):
        acc_ref[mine, block * LANES : (block + 1) * LANES] = x_ref[pl.ds(block, rows, stride=blocks), :]


def fold(front):
    row_blocks, height, blocks, lanes = front.shape
    rows, cols = row_blocks * height, blocks * lanes
    return pl.pallas_call(
        functools.partial(fold_kernel, blocks),
        out_shape=jax.ShapeDtypeStruct((rows, cols), front.dtype),
        grid=(row_blocks,),
        in_specs=[pl.BlockSpec((height * blocks, lanes), lambda i: (i, 0))],
        out_specs=pl.BlockSpec(memory_space=pltpu.VMEM),
        compiler_params=pltpu.CompilerParams(vmem_limit_bytes=VMEM_LIMIT),
        cost_estimate=pl.CostEstimate(flops=0, bytes_accessed=4 * front.size, transcendentals=0),
        name="fold",
    )(front.reshape(rows * blocks, lanes))


def one_kernel(count, scalars, acc_ref, high_ref, low_ref, *refs):
    slot = refs[:count]
    out_ref, buffer, sem, left_high, left_low = refs[count:]
    row_blocks, width, height = buffer.shape
    cut = acc_ref.shape[1] // pl.num_programs(0)
    step = pl.program_id(0)

    @pl.when(step == 0)
    def _():
        fetch(slot, scalars[1], (0, 0), buffer, sem).wait()
        for block in range(row_blocks):
            high, low = split(buffer[block].T)
            left_high[block * height : (block + 1) * height, :] = high
            left_low[block * height : (block + 1) * height, :] = low

    pivots = pl.ds(pl.multiple_of(scalars[0] * width, width), width)
    lanes = pl.ds(pl.multiple_of(step * cut, cut), cut)
    out_ref[:, lanes] = acc_ref[:, lanes] - product(
        left_high[...], left_low[...], high_ref[pivots, lanes], low_ref[pivots, lanes]
    )


def one(acc, slot, scalars, right):
    rows, cols = acc.shape
    width = slot[0].shape[1]
    cut = min(cols, 2 * LANES)
    resident = pl.BlockSpec(memory_space=pltpu.VMEM)
    return pl.pallas_call(
        functools.partial(one_kernel, len(slot)),
        out_shape=jax.ShapeDtypeStruct(acc.shape, acc.dtype),
        grid_spec=pltpu.PrefetchScalarGridSpec(
            num_scalar_prefetch=1,
            grid=(cols // cut,),
            in_specs=[resident] * 3 + [pl.BlockSpec(memory_space=pl.ANY)] * len(slot),
            out_specs=resident,
            scratch_shapes=[
                pltpu.VMEM(slot[0].shape, jnp.float32),
                pltpu.SemaphoreType.DMA,
                pltpu.VMEM((rows, width), jnp.bfloat16),
                pltpu.VMEM((rows, width), jnp.bfloat16),
            ],
        ),
        input_output_aliases={1: 0},
        compiler_params=pltpu.CompilerParams(vmem_limit_bytes=VMEM_LIMIT),
        cost_estimate=pl.CostEstimate(flops=6 * rows * width * cols, bytes_accessed=4 * slot[0].size, transcendentals=0),
        name="one",
    )(scalars, acc, right[0], right[1], *slot)


def last_kernel(blocks, count, first, base, scalars, acc_ref, high_ref, low_ref, *refs):
    slot = refs[:count]
    out_ref, _, buffer, sem = refs[-4:]
    _, width, height = buffer.shape
    rows = out_ref.shape[0] // blocks
    row_blocks = rows // height
    step = pl.program_id(0)

    @pl.when(step == 0)
    def _():
        fetch(slot, scalars[1], first, buffer, sem).wait()

    parts = [split(buffer[step * row_blocks + block].T) for block in range(row_blocks)]
    left_high = jnp.concatenate([part[0] for part in parts], axis=0)
    left_low = jnp.concatenate([part[1] for part in parts], axis=0)
    pivots = pl.ds(pl.multiple_of(scalars[0] * width, width), width)
    mine = pl.ds(pl.multiple_of(base + step * rows, rows), rows)
    pair = min(blocks, 2)
    for block in range(0, blocks, pair):
        lanes = pl.ds(block * LANES, pair * LANES)
        value = acc_ref[mine, lanes] - product(left_high, left_low, high_ref[pivots, lanes], low_ref[pivots, lanes])
        for one in range(pair):
            out_ref[pl.ds(block + one, rows, stride=blocks), :] = value[:, one * LANES : (one + 1) * LANES]


def last(acc, slot, first, scalars, right, blocks, first_block, row_blocks, buffer):
    rows, cols = acc.shape
    width, height = slot[0].shape[1:]
    step = 2 if row_blocks % 2 == 0 else 1
    base = first_block // step
    buffers = () if buffer is None else (buffer,)
    resident = pl.BlockSpec(memory_space=pltpu.VMEM)
    return pl.pallas_call(
        functools.partial(last_kernel, blocks, len(slot), first, first_block * height),
        out_shape=[
            jax.ShapeDtypeStruct((rows * blocks, LANES), acc.dtype),
            jax.ShapeDtypeStruct(acc.shape, acc.dtype),
        ],
        grid_spec=pltpu.PrefetchScalarGridSpec(
            num_scalar_prefetch=1,
            grid=(row_blocks // step,),
            in_specs=[resident] * 3 + [pl.BlockSpec(memory_space=pl.ANY)] * (len(slot) + len(buffers)),
            out_specs=[pl.BlockSpec((step * height * blocks, LANES), lambda i, s: (base + i, 0)), resident],
            scratch_shapes=[
                pltpu.VMEM((row_blocks, width, height), jnp.float32),
                pltpu.SemaphoreType.DMA,
            ],
        ),
        input_output_aliases={1: 1, 4 + len(slot): 0} if buffers else {1: 1},
        compiler_params=pltpu.CompilerParams(vmem_limit_bytes=VMEM_LIMIT),
        cost_estimate=pl.CostEstimate(
            flops=6 * row_blocks * height * width * cols, bytes_accessed=4 * row_blocks * height * cols, transcendentals=0
        ),
        name="last",
    )(scalars, acc, right[0], right[1], *slot, *buffers)


def moves(count):
    power = count & (count - 1) == 0
    pairs = lambda m: [(i, i ^ m if power else (i + m) % count) for i in range(count)]
    source = lambda me, m: me ^ m if power else lax.rem(me + count - m, count)
    target = lambda me, m: me ^ m if power else lax.rem(me + m, count)
    return power, pairs, source, target


def line(piece, axis, count, tails):
    mate = lambda i, odd: i + 1 if i % 2 == odd else i - 1
    reach = lambda i, odd: count - 1 - i if i % 2 == odd else i
    streams = {0: [], 1: []}
    for step in range(1, count):
        new = {}
        for odd in (0, 1):
            pairs = [(mate(i, odd), i) for i in range(count) if reach(i, odd) >= step]
            if pairs:
                what = piece if step == 1 else streams[1 - odd][step - 2]
                if tails > 1 and odd == 0 and step == count - 1:
                    cut = what.shape[0] // tails
                    new[odd] = [lax.ppermute(what[n * cut : (n + 1) * cut], axis, pairs) for n in range(tails)]
                else:
                    new[odd] = lax.ppermute(what, axis, pairs)
        for odd, value in new.items():
            streams[odd].append(value)
    return streams


def local(sizes, contribution, left_panel, right_panel):
    n_row, n_col, n_kk = sizes["row"], sizes["col"], sizes["kk"]
    row, col, kk = lax.axis_index("row"), lax.axis_index("col"), lax.axis_index("kk")
    row_blocks, height, blocks, lanes = contribution.shape
    cols = blocks * lanes
    width = left_panel.shape[3]
    depth = right_panel.shape[1]
    quarter = depth * n_row
    order = sorted(range(n_kk), key=lambda m: (bin(m).count("1"), m))

    power, pairs, _, target = moves(n_kk)
    left = left_panel.transpose(0, 2, 3, 1).reshape(n_kk, row_blocks, width, height)
    group = lambda index: lax.dynamic_index_in_dim(left, index, 0, keepdims=False)
    pieces = [group(kk) if m == 0 else lax.ppermute(group(target(kk, m)), "kk", pairs(m)) for m in order]

    tails = 2 if row_blocks % 2 == 0 and n_col > 2 else 1
    streams = [line(piece, "col", n_col, tails if i == n_kk - 1 else 0) for i, piece in enumerate(pieces)]
    even = col % 2 == 0
    length = jnp.where(even, n_col - 1 - col, col)
    lengths = sorted({n_col - 1 - i if i % 2 == 0 else i for i in range(n_col)})

    def slot_of(piece, stream, index):
        if index == 0:
            return (piece,)
        near, far = stream[0], stream[1]
        options = [(reach, far[index - 1 - reach]) for reach in lengths if index > reach]
        if not options:
            return (near[index - 1],)
        value = options[-1][1]
        for reach, other in options[:-1]:
            value = jnp.where(length == reach, other, value)
        return (near[index - 1], value) if index <= lengths[-1] else (value,)

    def scalars_of(index):
        if index == 0:
            return [col, jnp.int32(1)]
        past = index - length
        by_near = jnp.where(even, col + index, col - index)
        by_far = jnp.where(even, col - past, col + past)
        is_near = index <= length
        return [jnp.where(is_near, by_near, by_far), is_near.astype(jnp.int32)]

    own = right_panel.reshape(depth, cols)
    parts = {0: [own]}
    for m in order:
        bits = [1 << b for b in range(n_kk.bit_length()) if m >> b & 1]
        if m == 0:
            continue
        if not power or len(bits) == 1:
            parts[m] = [lax.ppermute(own, "kk", pairs(m))]
        else:
            half = depth // 2
            whole = lambda piece: piece[0] if len(piece) == 1 else jnp.concatenate(piece, axis=0)
            first = lax.ppermute(whole(parts[m ^ bits[0]])[:half], "kk", pairs(bits[0]))
            second = lax.ppermute(whole(parts[m ^ bits[-1]])[half:], "kk", pairs(bits[-1]))
            parts[m] = [first, second]

    row_power, row_pairs, row_source, _ = moves(n_row)
    rights = []
    for i, m in enumerate(order):
        rights.append(list(parts[m]))
        for j in range(1, n_row):
            rights[i] += [lax.ppermute(part, "row", row_pairs(j)) for part in parts[m]]
    if depth % width == 0:
        per = depth // width

        def place(shard):
            rank = shard // per
            return (rank ^ row if row_power else lax.rem(row - rank + n_row, n_row)) * per + lax.rem(shard, per)

    else:
        place = lambda shard: shard
        for i, right in enumerate(rights):
            count = len(right) // n_row
            total = jnp.zeros((quarter, cols), jnp.float32)
            for j in range(n_row):
                piece = jnp.concatenate(right[j * count : (j + 1) * count], axis=0)
                rank = row if j == 0 else row_source(row, j)
                total = lax.dynamic_update_slice_in_dim(total, piece, rank * depth, 0)
            rights[i] = [total]

    scalars = []
    for index in range(n_col):
        shard, flag = scalars_of(index)
        scalars += [place(shard), flag]
    scalars = jnp.stack(scalars).astype(jnp.int32)

    acc = fold(contribution)
    final = n_kk - 1
    early = max(n_col - 2, 1)
    for i in [*range(final - 1), final, final - 1]:
        slots = [slot_of(pieces[i], streams[i], index) for index in range(early if i == final else n_col)]
        acc, *terms = add(acc, slots, scalars, rights[i], i == final)
        if terms:
            kept = terms
    for index in range(early, n_col - 1):
        slot = slot_of(pieces[final], streams[final], index)
        acc = one(acc, slot, scalars[2 * index : 2 * index + 2], kept)

    cut = row_blocks // tails
    out = None
    for part in range(tails):
        stream = {0: list(streams[final][0]), 1: streams[final][1]}
        stream[0][-1] = stream[0][-1][part] if isinstance(stream[0][-1], list) else stream[0][-1]
        options = slot_of(pieces[final], stream, n_col - 1)
        first = [0 if option.shape[0] == cut else part * cut for option in options]
        out, acc = last(acc, options, first, scalars[-2:], kept, blocks, part * cut, cut, out)
    return out.reshape(contribution.shape)


def solution(mesh):
    placed = (P("kk", "row", None, "col"), P(None, "row", "kk", "col"), P("kk", "row", None, "col"))

    def body(*args):
        return local(dict(mesh.shape), *args)

    return jax.shard_map(
        body, mesh=mesh, in_specs=placed, out_specs=P("kk", "row", None, "col"), check_vma=False
    )
```

```python
import functools

import jax
import jax.numpy as jnp
from jax import lax
from jax.experimental import pallas as pl
from jax.experimental.pallas import tpu as pltpu
from jax.sharding import PartitionSpec as P


LANES = 128
VMEM_LIMIT = 16 * 1024 * 1024


def split(value):
    high = value.astype(jnp.bfloat16)
    return high, (value - high.astype(jnp.float32)).astype(jnp.bfloat16)


def product(left_high, left_low, right_high, right_low):
    dot = functools.partial(jnp.dot, preferred_element_type=jnp.float32)
    return dot(left_high, right_high) + (dot(left_high, right_low) + dot(left_low, right_high))


def fetch(slot, flag, first, buffer, sem):
    count = buffer.shape[0]
    copies = []
    for ref, skip in zip(slot, first):
        copies.append(pltpu.make_async_copy(ref.at[pl.ds(skip, count)], buffer, sem))
    if len(copies) == 1:
        copies[0].start()
    else:
        pl.when(flag != 0)(copies[0].start)
        pl.when(flag == 0)(copies[1].start)
    return copies[0]


def add_kernel(counts, pieces, keep, scalars, acc_ref, *refs):
    right, refs = refs[:pieces], refs[pieces:]
    slots = []
    for count in counts:
        slots.append(refs[:count])
        refs = refs[count:]
    out_ref, right_high, right_low, buffers, sems, turned, left_high, left_low = refs
    width, rows = slots[0][0].shape[1:]
    row_blocks = buffers.shape[1]
    cut = right[0].shape[1]
    step = pl.program_id(0)
    lanes = pl.ds(pl.multiple_of(step * cut, cut), cut)
    mine = lanes if keep else slice(None)

    def copies(start):
        for index, slot in enumerate(slots):
            if start:
                fetch(slot, scalars[2 * index + 1], (0, 0), buffers.at[index], sems.at[index])
            else:
                pltpu.make_async_copy(slot[0].at[pl.ds(0, row_blocks)], buffers.at[index], sems.at[index]).wait()

    @pl.when(step == 0)
    def _():
        copies(True)
        turned[...] = jnp.zeros_like(turned)

    at = 0
    for piece in right:
        high, low = split(piece[...])
        right_high[at : at + piece.shape[0], mine] = high
        right_low[at : at + piece.shape[0], mine] = low
        at += piece.shape[0]

    @pl.when(step == 0)
    def _():
        copies(False)

        def one(block, carry):
            for index in range(len(slots)):
                at = pl.multiple_of(scalars[2 * index] * width, width)
                turned[pl.ds(at, width), :] = buffers[index, block]
            high, low = split(turned[...].T)
            at = pl.multiple_of(block * rows, rows)
            left_high[pl.ds(at, rows), :] = high
            left_low[pl.ds(at, rows), :] = low
            return carry

        lax.fori_loop(0, row_blocks, one, 0)

    out_ref[:, lanes] = acc_ref[:, lanes] - product(
        left_high[...], left_low[...], right_high[:, mine], right_low[:, mine]
    )


def add(acc, slots, scalars, right, keep):
    rows, cols = acc.shape
    depth = sum(piece.shape[0] for piece in right)
    flat = [array for slot in slots for array in slot]
    cut = min(cols, 2 * LANES)
    resident = pl.BlockSpec(memory_space=pltpu.VMEM)
    used = len(slots) * flat[0].shape[1]
    shape = jax.ShapeDtypeStruct((depth, cols), jnp.bfloat16)
    terms = [pltpu.VMEM((depth, cut), jnp.bfloat16)] * 2
    return pl.pallas_call(
        functools.partial(add_kernel, [len(slot) for slot in slots], len(right), keep),
        out_shape=[jax.ShapeDtypeStruct(acc.shape, acc.dtype)] + [shape, shape] * keep,
        grid_spec=pltpu.PrefetchScalarGridSpec(
            num_scalar_prefetch=1,
            grid=(cols // cut,),
            in_specs=[resident]
            + [pl.BlockSpec((piece.shape[0], cut), lambda i, s: (0, i)) for piece in right]
            + [pl.BlockSpec(memory_space=pl.ANY)] * len(flat),
            out_specs=[resident] + [resident] * (2 * keep),
            scratch_shapes=terms * (not keep)
            + [
                pltpu.VMEM((len(slots),) + flat[0].shape, jnp.float32),
                pltpu.SemaphoreType.DMA((len(slots),)),
                pltpu.VMEM((depth, flat[0].shape[2]), jnp.float32),
                pltpu.VMEM((rows, depth), jnp.bfloat16),
                pltpu.VMEM((rows, depth), jnp.bfloat16),
            ],
        ),
        input_output_aliases={1: 0},
        compiler_params=pltpu.CompilerParams(vmem_limit_bytes=VMEM_LIMIT),
        cost_estimate=pl.CostEstimate(
            flops=6 * rows * used * cols, bytes_accessed=4 * depth * cols, transcendentals=0
        ),
        name="add",
    )(scalars, acc, *right, *flat)


def fold_kernel(blocks, x_ref, acc_ref):
    rows = x_ref.shape[0] // blocks
    mine = pl.ds(pl.multiple_of(pl.program_id(0) * rows, rows), rows)
    for block in range(blocks):
        acc_ref[mine, block * LANES : (block + 1) * LANES] = x_ref[pl.ds(block, rows, stride=blocks), :]


def fold(front):
    row_blocks, height, blocks, lanes = front.shape
    rows, cols = row_blocks * height, blocks * lanes
    return pl.pallas_call(
        functools.partial(fold_kernel, blocks),
        out_shape=jax.ShapeDtypeStruct((rows, cols), front.dtype),
        grid=(row_blocks,),
        in_specs=[pl.BlockSpec((height * blocks, lanes), lambda i: (i, 0))],
        out_specs=pl.BlockSpec(memory_space=pltpu.VMEM),
        compiler_params=pltpu.CompilerParams(vmem_limit_bytes=VMEM_LIMIT),
        cost_estimate=pl.CostEstimate(flops=0, bytes_accessed=4 * front.size, transcendentals=0),
        name="fold",
    )(front.reshape(rows * blocks, lanes))


def one_kernel(count, scalars, acc_ref, high_ref, low_ref, *refs):
    slot = refs[:count]
    out_ref, buffer, sem, left_high, left_low = refs[count:]
    row_blocks, width, height = buffer.shape
    cut = acc_ref.shape[1] // pl.num_programs(0)
    step = pl.program_id(0)

    @pl.when(step == 0)
    def _():
        fetch(slot, scalars[1], (0, 0), buffer, sem).wait()
        for block in range(row_blocks):
            high, low = split(buffer[block].T)
            left_high[block * height : (block + 1) * height, :] = high
            left_low[block * height : (block + 1) * height, :] = low

    pivots = pl.ds(pl.multiple_of(scalars[0] * width, width), width)
    lanes = pl.ds(pl.multiple_of(step * cut, cut), cut)
    out_ref[:, lanes] = acc_ref[:, lanes] - product(
        left_high[...], left_low[...], high_ref[pivots, lanes], low_ref[pivots, lanes]
    )


def one(acc, slot, scalars, right):
    rows, cols = acc.shape
    width = slot[0].shape[1]
    cut = min(cols, 2 * LANES)
    resident = pl.BlockSpec(memory_space=pltpu.VMEM)
    return pl.pallas_call(
        functools.partial(one_kernel, len(slot)),
        out_shape=jax.ShapeDtypeStruct(acc.shape, acc.dtype),
        grid_spec=pltpu.PrefetchScalarGridSpec(
            num_scalar_prefetch=1,
            grid=(cols // cut,),
            in_specs=[resident] * 3 + [pl.BlockSpec(memory_space=pl.ANY)] * len(slot),
            out_specs=resident,
            scratch_shapes=[
                pltpu.VMEM(slot[0].shape, jnp.float32),
                pltpu.SemaphoreType.DMA,
                pltpu.VMEM((rows, width), jnp.bfloat16),
                pltpu.VMEM((rows, width), jnp.bfloat16),
            ],
        ),
        input_output_aliases={1: 0},
        compiler_params=pltpu.CompilerParams(vmem_limit_bytes=VMEM_LIMIT),
        cost_estimate=pl.CostEstimate(flops=6 * rows * width * cols, bytes_accessed=4 * slot[0].size, transcendentals=0),
        name="one",
    )(scalars, acc, right[0], right[1], *slot)


def last_kernel(blocks, count, first, base, scalars, acc_ref, high_ref, low_ref, *refs):
    slot = refs[:count]
    out_ref, _, buffer, sem = refs[-4:]
    _, width, height = buffer.shape
    rows = out_ref.shape[0] // blocks
    row_blocks = rows // height
    step = pl.program_id(0)

    @pl.when(step == 0)
    def _():
        fetch(slot, scalars[1], first, buffer, sem).wait()

    parts = [split(buffer[step * row_blocks + block].T) for block in range(row_blocks)]
    left_high = jnp.concatenate([part[0] for part in parts], axis=0)
    left_low = jnp.concatenate([part[1] for part in parts], axis=0)
    pivots = pl.ds(pl.multiple_of(scalars[0] * width, width), width)
    mine = pl.ds(pl.multiple_of(base + step * rows, rows), rows)
    pair = min(blocks, 2)
    for block in range(0, blocks, pair):
        lanes = pl.ds(block * LANES, pair * LANES)
        value = acc_ref[mine, lanes] - product(left_high, left_low, high_ref[pivots, lanes], low_ref[pivots, lanes])
        for one in range(pair):
            out_ref[pl.ds(block + one, rows, stride=blocks), :] = value[:, one * LANES : (one + 1) * LANES]


def last(acc, slot, first, scalars, right, blocks, first_block, row_blocks, buffer):
    rows, cols = acc.shape
    width, height = slot[0].shape[1:]
    step = 2 if row_blocks % 4 == 0 else 1
    base = first_block // step
    buffers = () if buffer is None else (buffer,)
    resident = pl.BlockSpec(memory_space=pltpu.VMEM)
    return pl.pallas_call(
        functools.partial(last_kernel, blocks, len(slot), first, first_block * height),
        out_shape=[
            jax.ShapeDtypeStruct((rows * blocks, LANES), acc.dtype),
            jax.ShapeDtypeStruct(acc.shape, acc.dtype),
        ],
        grid_spec=pltpu.PrefetchScalarGridSpec(
            num_scalar_prefetch=1,
            grid=(row_blocks // step,),
            in_specs=[resident] * 3 + [pl.BlockSpec(memory_space=pl.ANY)] * (len(slot) + len(buffers)),
            out_specs=[pl.BlockSpec((step * height * blocks, LANES), lambda i, s: (base + i, 0)), resident],
            scratch_shapes=[
                pltpu.VMEM((row_blocks, width, height), jnp.float32),
                pltpu.SemaphoreType.DMA,
            ],
        ),
        input_output_aliases={1: 1, 4 + len(slot): 0} if buffers else {1: 1},
        compiler_params=pltpu.CompilerParams(vmem_limit_bytes=VMEM_LIMIT),
        cost_estimate=pl.CostEstimate(
            flops=6 * row_blocks * height * width * cols, bytes_accessed=4 * row_blocks * height * cols, transcendentals=0
        ),
        name="last",
    )(scalars, acc, right[0], right[1], *slot, *buffers)


def moves(count):
    power = count & (count - 1) == 0
    pairs = lambda m: [(i, i ^ m if power else (i + m) % count) for i in range(count)]
    source = lambda me, m: me ^ m if power else lax.rem(me + count - m, count)
    target = lambda me, m: me ^ m if power else lax.rem(me + m, count)
    return power, pairs, source, target


def line(piece, axis, count, tails):
    mate = lambda i, odd: i + 1 if i % 2 == odd else i - 1
    reach = lambda i, odd: count - 1 - i if i % 2 == odd else i
    streams = {0: [], 1: []}
    for step in range(1, count):
        new = {}
        for odd in (0, 1):
            pairs = [(mate(i, odd), i) for i in range(count) if reach(i, odd) >= step]
            if pairs:
                what = piece if step == 1 else streams[1 - odd][step - 2]
                if len(tails) > 1 and odd == 0 and step == count - 1:
                    parts = [what[sum(tails[:n]) : sum(tails[: n + 1])] for n in range(len(tails))]
                    new[odd] = [lax.ppermute(part, axis, pairs) for part in parts]
                else:
                    new[odd] = lax.ppermute(what, axis, pairs)
        for odd, value in new.items():
            streams[odd].append(value)
    return streams


def local(sizes, contribution, left_panel, right_panel):
    n_row, n_col, n_kk = sizes["row"], sizes["col"], sizes["kk"]
    row, col, kk = lax.axis_index("row"), lax.axis_index("col"), lax.axis_index("kk")
    row_blocks, height, blocks, lanes = contribution.shape
    cols = blocks * lanes
    width = left_panel.shape[3]
    depth = right_panel.shape[1]
    quarter = depth * n_row
    order = sorted(range(n_kk), key=lambda m: (bin(m).count("1"), m))

    power, pairs, _, target = moves(n_kk)
    left = left_panel.transpose(0, 2, 3, 1).reshape(n_kk, row_blocks, width, height)
    group = lambda index: lax.dynamic_index_in_dim(left, index, 0, keepdims=False)
    groups = [group(kk)] + [group(target(kk, m)) for m in order[1:2]]
    *groups, left = lax.optimization_barrier((*groups, left))
    groups += [group(target(kk, m)) for m in order[2:]]
    pieces = [groups[0] if m == 0 else lax.ppermute(groups[i], "kk", pairs(m)) for i, m in enumerate(order)]

    tails = [row_blocks // n for n in (2, 4, 4)] if row_blocks % 4 == 0 and n_col > 2 else [row_blocks]
    streams = [line(piece, "col", n_col, tails if i == n_kk - 1 else ()) for i, piece in enumerate(pieces)]
    even = col % 2 == 0
    length = jnp.where(even, n_col - 1 - col, col)
    lengths = sorted({n_col - 1 - i if i % 2 == 0 else i for i in range(n_col)})

    def slot_of(piece, stream, index):
        if index == 0:
            return (piece,)
        near, far = stream[0], stream[1]
        options = [(reach, far[index - 1 - reach]) for reach in lengths if index > reach]
        if not options:
            return (near[index - 1],)
        value = options[-1][1]
        for reach, other in options[:-1]:
            value = jnp.where(length == reach, other, value)
        return (near[index - 1], value) if index <= lengths[-1] else (value,)

    def scalars_of(index):
        if index == 0:
            return [col, jnp.int32(1)]
        past = index - length
        by_near = jnp.where(even, col + index, col - index)
        by_far = jnp.where(even, col - past, col + past)
        is_near = index <= length
        return [jnp.where(is_near, by_near, by_far), is_near.astype(jnp.int32)]

    own = right_panel.reshape(depth, cols)
    parts = {0: [own]}
    for m in order:
        bits = [1 << b for b in range(n_kk.bit_length()) if m >> b & 1]
        if m == 0:
            continue
        if not power or len(bits) == 1:
            parts[m] = [lax.ppermute(own, "kk", pairs(m))]
        else:
            half = depth // 2
            whole = lambda piece: piece[0] if len(piece) == 1 else jnp.concatenate(piece, axis=0)
            first = lax.ppermute(whole(parts[m ^ bits[0]])[:half], "kk", pairs(bits[0]))
            second = lax.ppermute(whole(parts[m ^ bits[-1]])[half:], "kk", pairs(bits[-1]))
            parts[m] = [first, second]

    row_power, row_pairs, row_source, _ = moves(n_row)
    rights = []
    for i, m in enumerate(order):
        rights.append(list(parts[m]))
        for j in range(1, n_row):
            rights[i] += [lax.ppermute(part, "row", row_pairs(j)) for part in parts[m]]
    if depth % width == 0:
        per = depth // width

        def place(shard):
            rank = shard // per
            return (rank ^ row if row_power else lax.rem(row - rank + n_row, n_row)) * per + lax.rem(shard, per)

    else:
        place = lambda shard: shard
        for i, right in enumerate(rights):
            count = len(right) // n_row
            total = jnp.zeros((quarter, cols), jnp.float32)
            for j in range(n_row):
                piece = jnp.concatenate(right[j * count : (j + 1) * count], axis=0)
                rank = row if j == 0 else row_source(row, j)
                total = lax.dynamic_update_slice_in_dim(total, piece, rank * depth, 0)
            rights[i] = [total]

    scalars = []
    for index in range(n_col):
        shard, flag = scalars_of(index)
        scalars += [place(shard), flag]
    scalars = jnp.stack(scalars).astype(jnp.int32)

    acc = fold(contribution)
    final = n_kk - 1
    early = max(n_col - 2, 1)
    for i in [*range(final - 1), final, final - 1]:
        slots = [slot_of(pieces[i], streams[i], index) for index in range(early if i == final else n_col)]
        acc, *terms = add(acc, slots, scalars, rights[i], i == final)
        if terms:
            kept = terms
    for index in range(early, n_col - 1):
        slot = slot_of(pieces[final], streams[final], index)
        acc = one(acc, slot, scalars[2 * index : 2 * index + 2], kept)

    out, start = None, 0
    for part, count in enumerate(tails):
        stream = {0: list(streams[final][0]), 1: streams[final][1]}
        if len(tails) > 1:
            stream[0][-1] = stream[0][-1][part]
        options = slot_of(pieces[final], stream, n_col - 1)
        first = [0 if option.shape[0] == count else start for option in options]
        out, acc = last(acc, options, first, scalars[-2:], kept, blocks, start, count, out)
        start += count
    return out.reshape(contribution.shape)


def solution(mesh):
    placed = (P("kk", "row", None, "col"), P(None, "row", "kk", "col"), P("kk", "row", None, "col"))

    def body(*args):
        return local(dict(mesh.shape), *args)

    return jax.shard_map(
        body, mesh=mesh, in_specs=placed, out_specs=P("kk", "row", None, "col"), check_vma=False
    )
```

```python
import functools

import jax
import jax.numpy as jnp
from jax import lax
from jax.experimental import pallas as pl
from jax.experimental.pallas import tpu as pltpu
from jax.sharding import PartitionSpec as P


LANES = 128
VMEM_LIMIT = 16 * 1024 * 1024


def split(value):
    high = value.astype(jnp.bfloat16)
    return high, (value - high.astype(jnp.float32)).astype(jnp.bfloat16)


def product(left_high, left_low, right_high, right_low):
    dot = functools.partial(jnp.dot, preferred_element_type=jnp.float32)
    return dot(left_high, right_high) + (dot(left_high, right_low) + dot(left_low, right_high))


def fetch(slot, flag, first, buffer, sem):
    count = buffer.shape[0]
    copies = []
    for ref, skip in zip(slot, first):
        copies.append(pltpu.make_async_copy(ref.at[pl.ds(skip, count)], buffer, sem))
    if len(copies) == 1:
        copies[0].start()
    else:
        pl.when(flag != 0)(copies[0].start)
        pl.when(flag == 0)(copies[1].start)
    return copies[0]


def add_kernel(counts, pieces, keep, scalars, acc_ref, *refs):
    right, refs = refs[:pieces], refs[pieces:]
    slots = []
    for count in counts:
        slots.append(refs[:count])
        refs = refs[count:]
    out_ref, right_high, right_low, buffers, sems, turned, left_high, left_low = refs
    width, rows = slots[0][0].shape[1:]
    row_blocks = buffers.shape[1]
    cut = right[0].shape[1]
    step = pl.program_id(0)
    lanes = pl.ds(pl.multiple_of(step * cut, cut), cut)
    mine = lanes if keep else slice(None)

    def copies(start):
        for index, slot in enumerate(slots):
            if start:
                fetch(slot, scalars[2 * index + 1], (0, 0), buffers.at[index], sems.at[index])
            else:
                pltpu.make_async_copy(slot[0].at[pl.ds(0, row_blocks)], buffers.at[index], sems.at[index]).wait()

    @pl.when(step == 0)
    def _():
        copies(True)
        turned[...] = jnp.zeros_like(turned)

    at = 0
    for piece in right:
        high, low = split(piece[...])
        right_high[at : at + piece.shape[0], mine] = high
        right_low[at : at + piece.shape[0], mine] = low
        at += piece.shape[0]

    @pl.when(step == 0)
    def _():
        copies(False)

        def one(block, carry):
            for index in range(len(slots)):
                at = pl.multiple_of(scalars[2 * index] * width, width)
                turned[pl.ds(at, width), :] = buffers[index, block]
            high, low = split(turned[...].T)
            at = pl.multiple_of(block * rows, rows)
            left_high[pl.ds(at, rows), :] = high
            left_low[pl.ds(at, rows), :] = low
            return carry

        lax.fori_loop(0, row_blocks, one, 0)

    out_ref[:, lanes] = acc_ref[:, lanes] - product(
        left_high[...], left_low[...], right_high[:, mine], right_low[:, mine]
    )


def add(acc, slots, scalars, right, keep):
    rows, cols = acc.shape
    depth = sum(piece.shape[0] for piece in right)
    flat = [array for slot in slots for array in slot]
    cut = min(cols, 2 * LANES)
    resident = pl.BlockSpec(memory_space=pltpu.VMEM)
    used = len(slots) * flat[0].shape[1]
    shape = jax.ShapeDtypeStruct((depth, cols), jnp.bfloat16)
    terms = [pltpu.VMEM((depth, cut), jnp.bfloat16)] * 2
    return pl.pallas_call(
        functools.partial(add_kernel, [len(slot) for slot in slots], len(right), keep),
        out_shape=[jax.ShapeDtypeStruct(acc.shape, acc.dtype)] + [shape, shape] * keep,
        grid_spec=pltpu.PrefetchScalarGridSpec(
            num_scalar_prefetch=1,
            grid=(cols // cut,),
            in_specs=[resident]
            + [pl.BlockSpec((piece.shape[0], cut), lambda i, s: (0, i)) for piece in right]
            + [pl.BlockSpec(memory_space=pl.ANY)] * len(flat),
            out_specs=[resident] + [resident] * (2 * keep),
            scratch_shapes=terms * (not keep)
            + [
                pltpu.VMEM((len(slots),) + flat[0].shape, jnp.float32),
                pltpu.SemaphoreType.DMA((len(slots),)),
                pltpu.VMEM((depth, flat[0].shape[2]), jnp.float32),
                pltpu.VMEM((rows, depth), jnp.bfloat16),
                pltpu.VMEM((rows, depth), jnp.bfloat16),
            ],
        ),
        input_output_aliases={1: 0},
        compiler_params=pltpu.CompilerParams(vmem_limit_bytes=VMEM_LIMIT),
        cost_estimate=pl.CostEstimate(
            flops=6 * rows * used * cols, bytes_accessed=4 * depth * cols, transcendentals=0
        ),
        name="add",
    )(scalars, acc, *right, *flat)


def fold_kernel(blocks, x_ref, acc_ref):
    rows = x_ref.shape[0] // blocks
    mine = pl.ds(pl.multiple_of(pl.program_id(0) * rows, rows), rows)
    for block in range(blocks):
        acc_ref[mine, block * LANES : (block + 1) * LANES] = x_ref[pl.ds(block, rows, stride=blocks), :]


def fold(front):
    row_blocks, height, blocks, lanes = front.shape
    rows, cols = row_blocks * height, blocks * lanes
    return pl.pallas_call(
        functools.partial(fold_kernel, blocks),
        out_shape=jax.ShapeDtypeStruct((rows, cols), front.dtype),
        grid=(row_blocks,),
        in_specs=[pl.BlockSpec((height * blocks, lanes), lambda i: (i, 0))],
        out_specs=pl.BlockSpec(memory_space=pltpu.VMEM),
        compiler_params=pltpu.CompilerParams(vmem_limit_bytes=VMEM_LIMIT),
        cost_estimate=pl.CostEstimate(flops=0, bytes_accessed=4 * front.size, transcendentals=0),
        name="fold",
    )(front.reshape(rows * blocks, lanes))


def one_kernel(count, scalars, acc_ref, high_ref, low_ref, *refs):
    slot = refs[:count]
    out_ref, buffer, sem, left_high, left_low = refs[count:]
    row_blocks, width, height = buffer.shape
    cut = acc_ref.shape[1] // pl.num_programs(0)
    step = pl.program_id(0)

    @pl.when(step == 0)
    def _():
        fetch(slot, scalars[1], (0, 0), buffer, sem).wait()
        for block in range(row_blocks):
            high, low = split(buffer[block].T)
            left_high[block * height : (block + 1) * height, :] = high
            left_low[block * height : (block + 1) * height, :] = low

    pivots = pl.ds(pl.multiple_of(scalars[0] * width, width), width)
    lanes = pl.ds(pl.multiple_of(step * cut, cut), cut)
    out_ref[:, lanes] = acc_ref[:, lanes] - product(
        left_high[...], left_low[...], high_ref[pivots, lanes], low_ref[pivots, lanes]
    )


def one(acc, slot, scalars, right):
    rows, cols = acc.shape
    width = slot[0].shape[1]
    cut = min(cols, 2 * LANES)
    resident = pl.BlockSpec(memory_space=pltpu.VMEM)
    return pl.pallas_call(
        functools.partial(one_kernel, len(slot)),
        out_shape=jax.ShapeDtypeStruct(acc.shape, acc.dtype),
        grid_spec=pltpu.PrefetchScalarGridSpec(
            num_scalar_prefetch=1,
            grid=(cols // cut,),
            in_specs=[resident] * 3 + [pl.BlockSpec(memory_space=pl.ANY)] * len(slot),
            out_specs=resident,
            scratch_shapes=[
                pltpu.VMEM(slot[0].shape, jnp.float32),
                pltpu.SemaphoreType.DMA,
                pltpu.VMEM((rows, width), jnp.bfloat16),
                pltpu.VMEM((rows, width), jnp.bfloat16),
            ],
        ),
        input_output_aliases={1: 0},
        compiler_params=pltpu.CompilerParams(vmem_limit_bytes=VMEM_LIMIT),
        cost_estimate=pl.CostEstimate(flops=6 * rows * width * cols, bytes_accessed=4 * slot[0].size, transcendentals=0),
        name="one",
    )(scalars, acc, right[0], right[1], *slot)


def last_kernel(blocks, count, first, base, scalars, acc_ref, high_ref, low_ref, *refs):
    slot = refs[:count]
    out_ref, _, buffer, sem = refs[-4:]
    _, width, height = buffer.shape
    rows = out_ref.shape[0] // blocks
    row_blocks = rows // height
    step = pl.program_id(0)

    @pl.when(step == 0)
    def _():
        fetch(slot, scalars[1], first, buffer, sem).wait()

    parts = [split(buffer[step * row_blocks + block].T) for block in range(row_blocks)]
    left_high = jnp.concatenate([part[0] for part in parts], axis=0)
    left_low = jnp.concatenate([part[1] for part in parts], axis=0)
    left_both = jnp.concatenate([left_high, left_low], axis=0)
    pivots = pl.ds(pl.multiple_of(scalars[0] * width, width), width)
    mine = pl.ds(pl.multiple_of(base + step * rows, rows), rows)
    pair = min(blocks, 2)
    for block in range(0, blocks, pair):
        lanes = pl.ds(block * LANES, pair * LANES)
        both = jnp.dot(left_both, high_ref[pivots, lanes], preferred_element_type=jnp.float32)
        rest = jnp.dot(left_high, low_ref[pivots, lanes], preferred_element_type=jnp.float32)
        value = acc_ref[mine, lanes] - (both[:rows] + (both[rows:] + rest))
        for one in range(pair):
            out_ref[pl.ds(block + one, rows, stride=blocks), :] = value[:, one * LANES : (one + 1) * LANES]


def last(acc, slot, first, scalars, right, blocks, first_block, row_blocks, buffer):
    rows, cols = acc.shape
    width, height = slot[0].shape[1:]
    step = 2 if row_blocks % 4 == 0 else 1
    base = first_block // step
    buffers = () if buffer is None else (buffer,)
    resident = pl.BlockSpec(memory_space=pltpu.VMEM)
    return pl.pallas_call(
        functools.partial(last_kernel, blocks, len(slot), first, first_block * height),
        out_shape=[
            jax.ShapeDtypeStruct((rows * blocks, LANES), acc.dtype),
            jax.ShapeDtypeStruct(acc.shape, acc.dtype),
        ],
        grid_spec=pltpu.PrefetchScalarGridSpec(
            num_scalar_prefetch=1,
            grid=(row_blocks // step,),
            in_specs=[resident] * 3 + [pl.BlockSpec(memory_space=pl.ANY)] * (len(slot) + len(buffers)),
            out_specs=[pl.BlockSpec((step * height * blocks, LANES), lambda i, s: (base + i, 0)), resident],
            scratch_shapes=[
                pltpu.VMEM((row_blocks, width, height), jnp.float32),
                pltpu.SemaphoreType.DMA,
            ],
        ),
        input_output_aliases={1: 1, 4 + len(slot): 0} if buffers else {1: 1},
        compiler_params=pltpu.CompilerParams(vmem_limit_bytes=VMEM_LIMIT),
        cost_estimate=pl.CostEstimate(
            flops=6 * row_blocks * height * width * cols, bytes_accessed=4 * row_blocks * height * cols, transcendentals=0
        ),
        name="last",
    )(scalars, acc, right[0], right[1], *slot, *buffers)


def moves(count):
    power = count & (count - 1) == 0
    pairs = lambda m: [(i, i ^ m if power else (i + m) % count) for i in range(count)]
    source = lambda me, m: me ^ m if power else lax.rem(me + count - m, count)
    target = lambda me, m: me ^ m if power else lax.rem(me + m, count)
    return power, pairs, source, target


def line(piece, axis, count, tails):
    mate = lambda i, odd: i + 1 if i % 2 == odd else i - 1
    reach = lambda i, odd: count - 1 - i if i % 2 == odd else i
    streams = {0: [], 1: []}
    for step in range(1, count):
        new = {}
        for odd in (0, 1):
            pairs = [(mate(i, odd), i) for i in range(count) if reach(i, odd) >= step]
            if pairs:
                what = piece if step == 1 else streams[1 - odd][step - 2]
                if len(tails) > 1 and odd == 0 and step == count - 1:
                    parts = [what[sum(tails[:n]) : sum(tails[: n + 1])] for n in range(len(tails))]
                    new[odd] = [lax.ppermute(part, axis, pairs) for part in parts]
                else:
                    new[odd] = lax.ppermute(what, axis, pairs)
        for odd, value in new.items():
            streams[odd].append(value)
    return streams


def local(sizes, contribution, left_panel, right_panel):
    n_row, n_col, n_kk = sizes["row"], sizes["col"], sizes["kk"]
    row, col, kk = lax.axis_index("row"), lax.axis_index("col"), lax.axis_index("kk")
    row_blocks, height, blocks, lanes = contribution.shape
    cols = blocks * lanes
    width = left_panel.shape[3]
    depth = right_panel.shape[1]
    quarter = depth * n_row
    order = sorted(range(n_kk), key=lambda m: (bin(m).count("1"), m))

    power, pairs, _, target = moves(n_kk)
    left = left_panel.transpose(0, 2, 3, 1).reshape(n_kk, row_blocks, width, height)
    group = lambda index: lax.dynamic_index_in_dim(left, index, 0, keepdims=False)
    groups = [group(kk)] + [group(target(kk, m)) for m in order[1:2]]
    *groups, left = lax.optimization_barrier((*groups, left))
    groups += [group(target(kk, m)) for m in order[2:]]
    pieces = [groups[0] if m == 0 else lax.ppermute(groups[i], "kk", pairs(m)) for i, m in enumerate(order)]

    tails = [(row_blocks + 2 - n) // 3 for n in range(3)] if row_blocks > 2 and n_col > 2 else [row_blocks]
    streams = [line(piece, "col", n_col, tails if i == n_kk - 1 else ()) for i, piece in enumerate(pieces)]
    even = col % 2 == 0
    length = jnp.where(even, n_col - 1 - col, col)
    lengths = sorted({n_col - 1 - i if i % 2 == 0 else i for i in range(n_col)})

    def slot_of(piece, stream, index):
        if index == 0:
            return (piece,)
        near, far = stream[0], stream[1]
        options = [(reach, far[index - 1 - reach]) for reach in lengths if index > reach]
        if not options:
            return (near[index - 1],)
        value = options[-1][1]
        for reach, other in options[:-1]:
            value = jnp.where(length == reach, other, value)
        return (near[index - 1], value) if index <= lengths[-1] else (value,)

    def scalars_of(index):
        if index == 0:
            return [col, jnp.int32(1)]
        past = index - length
        by_near = jnp.where(even, col + index, col - index)
        by_far = jnp.where(even, col - past, col + past)
        is_near = index <= length
        return [jnp.where(is_near, by_near, by_far), is_near.astype(jnp.int32)]

    own = right_panel.reshape(depth, cols)
    parts = {0: [own]}
    for m in order:
        bits = [1 << b for b in range(n_kk.bit_length()) if m >> b & 1]
        if m == 0:
            continue
        if not power or len(bits) == 1:
            parts[m] = [lax.ppermute(own, "kk", pairs(m))]
        else:
            half = depth // 2
            whole = lambda piece: piece[0] if len(piece) == 1 else jnp.concatenate(piece, axis=0)
            first = lax.ppermute(whole(parts[m ^ bits[0]])[:half], "kk", pairs(bits[0]))
            second = lax.ppermute(whole(parts[m ^ bits[-1]])[half:], "kk", pairs(bits[-1]))
            parts[m] = [first, second]

    row_power, row_pairs, row_source, _ = moves(n_row)
    rights = []
    for i, m in enumerate(order):
        rights.append(list(parts[m]))
        for j in range(1, n_row):
            rights[i] += [lax.ppermute(part, "row", row_pairs(j)) for part in parts[m]]
    if depth % width == 0:
        per = depth // width

        def place(shard):
            rank = shard // per
            return (rank ^ row if row_power else lax.rem(row - rank + n_row, n_row)) * per + lax.rem(shard, per)

    else:
        place = lambda shard: shard
        for i, right in enumerate(rights):
            count = len(right) // n_row
            total = jnp.zeros((quarter, cols), jnp.float32)
            for j in range(n_row):
                piece = jnp.concatenate(right[j * count : (j + 1) * count], axis=0)
                rank = row if j == 0 else row_source(row, j)
                total = lax.dynamic_update_slice_in_dim(total, piece, rank * depth, 0)
            rights[i] = [total]

    scalars = []
    for index in range(n_col):
        shard, flag = scalars_of(index)
        scalars += [place(shard), flag]
    scalars = jnp.stack(scalars).astype(jnp.int32)

    acc = fold(contribution)
    final = n_kk - 1
    early = max(n_col - 2, 1)
    for i in [*range(final - 1), final, final - 1]:
        slots = [slot_of(pieces[i], streams[i], index) for index in range(early if i == final else n_col)]
        acc, *terms = add(acc, slots, scalars, rights[i], i == final)
        if terms:
            kept = terms
    for index in range(early, n_col - 1):
        slot = slot_of(pieces[final], streams[final], index)
        acc = one(acc, slot, scalars[2 * index : 2 * index + 2], kept)

    out, start = None, 0
    for part, count in enumerate(tails):
        stream = {0: list(streams[final][0]), 1: streams[final][1]}
        if len(tails) > 1:
            stream[0][-1] = stream[0][-1][part]
        options = slot_of(pieces[final], stream, n_col - 1)
        first = [0 if option.shape[0] == count else start for option in options]
        out, acc = last(acc, options, first, scalars[-2:], kept, blocks, start, count, out)
        start += count
    return out.reshape(contribution.shape)


def solution(mesh):
    placed = (P("kk", "row", None, "col"), P(None, "row", "kk", "col"), P("kk", "row", None, "col"))

    def body(*args):
        return local(dict(mesh.shape), *args)

    return jax.shard_map(
        body, mesh=mesh, in_specs=placed, out_specs=P("kk", "row", None, "col"), check_vma=False
    )
```

```python
import functools

import jax
import jax.numpy as jnp
from jax import lax
from jax.experimental import pallas as pl
from jax.experimental.pallas import tpu as pltpu
from jax.sharding import PartitionSpec as P


LANES = 128
VMEM_LIMIT = 16 * 1024 * 1024


def split(value):
    high = value.astype(jnp.bfloat16)
    return high, (value - high.astype(jnp.float32)).astype(jnp.bfloat16)


def product(left_high, left_low, right_high, right_low):
    dot = functools.partial(jnp.dot, preferred_element_type=jnp.float32)
    return dot(left_high, right_high) + (dot(left_high, right_low) + dot(left_low, right_high))


def fetch(slot, flag, first, buffer, sem):
    count = buffer.shape[0]
    copies = []
    for ref, skip in zip(slot, first):
        copies.append(pltpu.make_async_copy(ref.at[pl.ds(skip, count)], buffer, sem))
    if len(copies) == 1:
        copies[0].start()
    else:
        pl.when(flag != 0)(copies[0].start)
        pl.when(flag == 0)(copies[1].start)
    return copies[0]


def add_kernel(counts, pieces, keep, scalars, acc_ref, *refs):
    right, refs = refs[:pieces], refs[pieces:]
    slots = []
    for count in counts:
        slots.append(refs[:count])
        refs = refs[count:]
    out_ref, right_high, right_low, buffers, sems, turned, left_high, left_low = refs
    width, rows = slots[0][0].shape[1:]
    row_blocks = buffers.shape[1]
    cut = right[0].shape[1]
    step = pl.program_id(0)
    lanes = pl.ds(pl.multiple_of(step * cut, cut), cut)
    mine = lanes if keep else slice(None)

    def copies(start):
        for index, slot in enumerate(slots):
            if start:
                fetch(slot, scalars[2 * index + 1], (0, 0), buffers.at[index], sems.at[index])
            else:
                pltpu.make_async_copy(slot[0].at[pl.ds(0, row_blocks)], buffers.at[index], sems.at[index]).wait()

    @pl.when(step == 0)
    def _():
        copies(True)
        turned[...] = jnp.zeros_like(turned)

    at = 0
    for piece in right:
        high, low = split(piece[...])
        right_high[at : at + piece.shape[0], mine] = high
        right_low[at : at + piece.shape[0], mine] = low
        at += piece.shape[0]

    @pl.when(step == 0)
    def _():
        copies(False)

        def one(block, carry):
            for index in range(len(slots)):
                at = pl.multiple_of(scalars[2 * index] * width, width)
                turned[pl.ds(at, width), :] = buffers[index, block]
            high, low = split(turned[...].T)
            at = pl.multiple_of(block * rows, rows)
            left_high[pl.ds(at, rows), :] = high
            left_low[pl.ds(at, rows), :] = low
            return carry

        lax.fori_loop(0, row_blocks, one, 0)

    out_ref[:, lanes] = acc_ref[:, lanes] - product(
        left_high[...], left_low[...], right_high[:, mine], right_low[:, mine]
    )


def add(acc, slots, scalars, right, keep):
    rows, cols = acc.shape
    depth = sum(piece.shape[0] for piece in right)
    flat = [array for slot in slots for array in slot]
    cut = min(cols, 2 * LANES)
    resident = pl.BlockSpec(memory_space=pltpu.VMEM)
    used = len(slots) * flat[0].shape[1]
    shape = jax.ShapeDtypeStruct((depth, cols), jnp.bfloat16)
    terms = [pltpu.VMEM((depth, cut), jnp.bfloat16)] * 2
    return pl.pallas_call(
        functools.partial(add_kernel, [len(slot) for slot in slots], len(right), keep),
        out_shape=[jax.ShapeDtypeStruct(acc.shape, acc.dtype)] + [shape, shape] * keep,
        grid_spec=pltpu.PrefetchScalarGridSpec(
            num_scalar_prefetch=1,
            grid=(cols // cut,),
            in_specs=[resident]
            + [pl.BlockSpec((piece.shape[0], cut), lambda i, s: (0, i)) for piece in right]
            + [pl.BlockSpec(memory_space=pl.ANY)] * len(flat),
            out_specs=[resident] + [resident] * (2 * keep),
            scratch_shapes=terms * (not keep)
            + [
                pltpu.VMEM((len(slots),) + flat[0].shape, jnp.float32),
                pltpu.SemaphoreType.DMA((len(slots),)),
                pltpu.VMEM((depth, flat[0].shape[2]), jnp.float32),
                pltpu.VMEM((rows, depth), jnp.bfloat16),
                pltpu.VMEM((rows, depth), jnp.bfloat16),
            ],
        ),
        input_output_aliases={1: 0},
        compiler_params=pltpu.CompilerParams(vmem_limit_bytes=VMEM_LIMIT),
        cost_estimate=pl.CostEstimate(
            flops=6 * rows * used * cols, bytes_accessed=4 * depth * cols, transcendentals=0
        ),
        name="add",
    )(scalars, acc, *right, *flat)


def fold_kernel(blocks, x_ref, acc_ref):
    rows = x_ref.shape[0] // blocks
    mine = pl.ds(pl.multiple_of(pl.program_id(0) * rows, rows), rows)
    for block in range(blocks):
        acc_ref[mine, block * LANES : (block + 1) * LANES] = x_ref[pl.ds(block, rows, stride=blocks), :]


def fold(front):
    row_blocks, height, blocks, lanes = front.shape
    rows, cols = row_blocks * height, blocks * lanes
    return pl.pallas_call(
        functools.partial(fold_kernel, blocks),
        out_shape=jax.ShapeDtypeStruct((rows, cols), front.dtype),
        grid=(row_blocks,),
        in_specs=[pl.BlockSpec((height * blocks, lanes), lambda i: (i, 0))],
        out_specs=pl.BlockSpec(memory_space=pltpu.VMEM),
        compiler_params=pltpu.CompilerParams(vmem_limit_bytes=VMEM_LIMIT),
        cost_estimate=pl.CostEstimate(flops=0, bytes_accessed=4 * front.size, transcendentals=0),
        name="fold",
    )(front.reshape(rows * blocks, lanes))


def one_kernel(count, scalars, acc_ref, high_ref, low_ref, *refs):
    slot = refs[:count]
    out_ref, buffer, sem, left_high, left_low = refs[count:]
    row_blocks, width, height = buffer.shape
    cut = acc_ref.shape[1] // pl.num_programs(0)
    step = pl.program_id(0)

    @pl.when(step == 0)
    def _():
        fetch(slot, scalars[1], (0, 0), buffer, sem).wait()
        for block in range(row_blocks):
            high, low = split(buffer[block].T)
            left_high[block * height : (block + 1) * height, :] = high
            left_low[block * height : (block + 1) * height, :] = low

    pivots = pl.ds(pl.multiple_of(scalars[0] * width, width), width)
    lanes = pl.ds(pl.multiple_of(step * cut, cut), cut)
    out_ref[:, lanes] = acc_ref[:, lanes] - product(
        left_high[...], left_low[...], high_ref[pivots, lanes], low_ref[pivots, lanes]
    )


def one(acc, slot, scalars, right):
    rows, cols = acc.shape
    width = slot[0].shape[1]
    cut = min(cols, 2 * LANES)
    resident = pl.BlockSpec(memory_space=pltpu.VMEM)
    return pl.pallas_call(
        functools.partial(one_kernel, len(slot)),
        out_shape=jax.ShapeDtypeStruct(acc.shape, acc.dtype),
        grid_spec=pltpu.PrefetchScalarGridSpec(
            num_scalar_prefetch=1,
            grid=(cols // cut,),
            in_specs=[resident] * 3 + [pl.BlockSpec(memory_space=pl.ANY)] * len(slot),
            out_specs=resident,
            scratch_shapes=[
                pltpu.VMEM(slot[0].shape, jnp.float32),
                pltpu.SemaphoreType.DMA,
                pltpu.VMEM((rows, width), jnp.bfloat16),
                pltpu.VMEM((rows, width), jnp.bfloat16),
            ],
        ),
        input_output_aliases={1: 0},
        compiler_params=pltpu.CompilerParams(vmem_limit_bytes=VMEM_LIMIT),
        cost_estimate=pl.CostEstimate(flops=6 * rows * width * cols, bytes_accessed=4 * slot[0].size, transcendentals=0),
        name="one",
    )(scalars, acc, right[0], right[1], *slot)


def last_kernel(blocks, count, first, base, scalars, acc_ref, high_ref, low_ref, *refs):
    slot = refs[:count]
    out_ref, _, buffer, sem = refs[-4:]
    _, width, height = buffer.shape
    rows = out_ref.shape[0] // blocks
    row_blocks = rows // height
    step = pl.program_id(0)

    @pl.when(step == 0)
    def _():
        fetch(slot, scalars[1], first, buffer, sem).wait()

    parts = [split(buffer[step * row_blocks + block].T) for block in range(row_blocks)]
    left_high = jnp.concatenate([part[0] for part in parts], axis=0)
    left_low = jnp.concatenate([part[1] for part in parts], axis=0)
    left_both = jnp.concatenate([left_high, left_low], axis=0)
    pivots = pl.ds(pl.multiple_of(scalars[0] * width, width), width)
    mine = pl.ds(pl.multiple_of(base + step * rows, rows), rows)
    pair = min(blocks, 2)
    for block in range(0, blocks, pair):
        lanes = pl.ds(block * LANES, pair * LANES)
        both = jnp.dot(left_both, high_ref[pivots, lanes], preferred_element_type=jnp.float32)
        rest = jnp.dot(left_high, low_ref[pivots, lanes], preferred_element_type=jnp.float32)
        value = acc_ref[mine, lanes] - (both[:rows] + (both[rows:] + rest))
        for one in range(pair):
            out_ref[pl.ds(block + one, rows, stride=blocks), :] = value[:, one * LANES : (one + 1) * LANES]


def last(acc, slot, first, scalars, right, blocks, first_block, row_blocks, buffer):
    rows, cols = acc.shape
    width, height = slot[0].shape[1:]
    step = 2 if row_blocks % 4 == 0 else 1
    base = first_block // step
    buffers = () if buffer is None else (buffer,)
    resident = pl.BlockSpec(memory_space=pltpu.VMEM)
    return pl.pallas_call(
        functools.partial(last_kernel, blocks, len(slot), first, first_block * height),
        out_shape=[
            jax.ShapeDtypeStruct((rows * blocks, LANES), acc.dtype),
            jax.ShapeDtypeStruct(acc.shape, acc.dtype),
        ],
        grid_spec=pltpu.PrefetchScalarGridSpec(
            num_scalar_prefetch=1,
            grid=(row_blocks // step,),
            in_specs=[resident] * 3 + [pl.BlockSpec(memory_space=pl.ANY)] * (len(slot) + len(buffers)),
            out_specs=[pl.BlockSpec((step * height * blocks, LANES), lambda i, s: (base + i, 0)), resident],
            scratch_shapes=[
                pltpu.VMEM((row_blocks, width, height), jnp.float32),
                pltpu.SemaphoreType.DMA,
            ],
        ),
        input_output_aliases={1: 1, 4 + len(slot): 0} if buffers else {1: 1},
        compiler_params=pltpu.CompilerParams(vmem_limit_bytes=VMEM_LIMIT),
        cost_estimate=pl.CostEstimate(
            flops=6 * row_blocks * height * width * cols, bytes_accessed=4 * row_blocks * height * cols, transcendentals=0
        ),
        name="last",
    )(scalars, acc, right[0], right[1], *slot, *buffers)


def moves(count):
    power = count & (count - 1) == 0
    pairs = lambda m: [(i, i ^ m if power else (i + m) % count) for i in range(count)]
    source = lambda me, m: me ^ m if power else lax.rem(me + count - m, count)
    target = lambda me, m: me ^ m if power else lax.rem(me + m, count)
    return power, pairs, source, target


def line(piece, axis, count, tails):
    mate = lambda i, odd: i + 1 if i % 2 == odd else i - 1
    reach = lambda i, odd: count - 1 - i if i % 2 == odd else i
    streams = {0: [], 1: []}
    for step in range(1, count):
        new = {}
        for odd in (0, 1):
            pairs = [(mate(i, odd), i) for i in range(count) if reach(i, odd) >= step]
            if pairs:
                what = piece if step == 1 else streams[1 - odd][step - 2]
                if len(tails) > 1 and odd == 0 and step == count - 1:
                    parts = [what[sum(tails[:n]) : sum(tails[: n + 1])] for n in range(len(tails))]
                    new[odd] = [lax.ppermute(part, axis, pairs) for part in parts]
                else:
                    new[odd] = lax.ppermute(what, axis, pairs)
        for odd, value in new.items():
            streams[odd].append(value)
    return streams


def local(sizes, contribution, left_panel, right_panel):
    n_row, n_col, n_kk = sizes["row"], sizes["col"], sizes["kk"]
    row, col, kk = lax.axis_index("row"), lax.axis_index("col"), lax.axis_index("kk")
    row_blocks, height, blocks, lanes = contribution.shape
    cols = blocks * lanes
    width = left_panel.shape[3]
    depth = right_panel.shape[1]
    quarter = depth * n_row
    order = sorted(range(n_kk), key=lambda m: (bin(m).count("1"), m))

    power, pairs, _, target = moves(n_kk)
    left = left_panel.transpose(0, 2, 3, 1).reshape(n_kk, row_blocks, width, height)
    group = lambda index: lax.dynamic_index_in_dim(left, index, 0, keepdims=False)
    pieces = [group(kk) if m == 0 else lax.ppermute(group(target(kk, m)), "kk", pairs(m)) for m in order]

    tails = [(row_blocks + 2 - n) // 3 for n in range(3)] if row_blocks > 2 and n_col > 2 else [row_blocks]
    streams = [line(piece, "col", n_col, tails if i == n_kk - 1 else ()) for i, piece in enumerate(pieces)]
    even = col % 2 == 0
    length = jnp.where(even, n_col - 1 - col, col)
    lengths = sorted({n_col - 1 - i if i % 2 == 0 else i for i in range(n_col)})

    def slot_of(piece, stream, index):
        if index == 0:
            return (piece,)
        near, far = stream[0], stream[1]
        options = [(reach, far[index - 1 - reach]) for reach in lengths if index > reach]
        if not options:
            return (near[index - 1],)
        value = options[-1][1]
        for reach, other in options[:-1]:
            value = jnp.where(length == reach, other, value)
        return (near[index - 1], value) if index <= lengths[-1] else (value,)

    def scalars_of(index):
        if index == 0:
            return [col, jnp.int32(1)]
        past = index - length
        by_near = jnp.where(even, col + index, col - index)
        by_far = jnp.where(even, col - past, col + past)
        is_near = index <= length
        return [jnp.where(is_near, by_near, by_far), is_near.astype(jnp.int32)]

    own = right_panel.reshape(depth, cols)
    parts = {0: [own]}
    for m in order:
        bits = [1 << b for b in range(n_kk.bit_length()) if m >> b & 1]
        if m == 0:
            continue
        if not power or len(bits) == 1:
            parts[m] = [lax.ppermute(own, "kk", pairs(m))]
        else:
            half = depth // 2
            whole = lambda piece: piece[0] if len(piece) == 1 else jnp.concatenate(piece, axis=0)
            first = lax.ppermute(whole(parts[m ^ bits[0]])[:half], "kk", pairs(bits[0]))
            second = lax.ppermute(whole(parts[m ^ bits[-1]])[half:], "kk", pairs(bits[-1]))
            parts[m] = [first, second]

    row_power, row_pairs, row_source, _ = moves(n_row)
    rights = []
    for i, m in enumerate(order):
        rights.append(list(parts[m]))
        for j in range(1, n_row):
            rights[i] += [lax.ppermute(part, "row", row_pairs(j)) for part in parts[m]]
    if depth % width == 0:
        per = depth // width

        def place(shard):
            rank = shard // per
            return (rank ^ row if row_power else lax.rem(row - rank + n_row, n_row)) * per + lax.rem(shard, per)

    else:
        place = lambda shard: shard
        for i, right in enumerate(rights):
            count = len(right) // n_row
            total = jnp.zeros((quarter, cols), jnp.float32)
            for j in range(n_row):
                piece = jnp.concatenate(right[j * count : (j + 1) * count], axis=0)
                rank = row if j == 0 else row_source(row, j)
                total = lax.dynamic_update_slice_in_dim(total, piece, rank * depth, 0)
            rights[i] = [total]

    scalars = []
    for index in range(n_col):
        shard, flag = scalars_of(index)
        scalars += [place(shard), flag]
    scalars = jnp.stack(scalars).astype(jnp.int32)

    acc = fold(contribution)
    final = n_kk - 1
    early = max(n_col - 2, 1)
    for i in [*range(final - 1), final, final - 1]:
        slots = [slot_of(pieces[i], streams[i], index) for index in range(early if i == final else n_col)]
        acc, *terms = add(acc, slots, scalars, rights[i], i == final)
        if terms:
            kept = terms
    for index in range(early, n_col - 1):
        slot = slot_of(pieces[final], streams[final], index)
        acc = one(acc, slot, scalars[2 * index : 2 * index + 2], kept)

    out, start = None, 0
    for part, count in enumerate(tails):
        stream = {0: list(streams[final][0]), 1: streams[final][1]}
        if len(tails) > 1:
            stream[0][-1] = stream[0][-1][part]
        options = slot_of(pieces[final], stream, n_col - 1)
        first = [0 if option.shape[0] == count else start for option in options]
        out, acc = last(acc, options, first, scalars[-2:], kept, blocks, start, count, out)
        start += count
    return out.reshape(contribution.shape)


def solution(mesh):
    placed = (P("kk", "row", None, "col"), P(None, "row", "kk", "col"), P("kk", "row", None, "col"))

    def body(*args):
        return local(dict(mesh.shape), *args)

    return jax.shard_map(
        body, mesh=mesh, in_specs=placed, out_specs=P("kk", "row", None, "col"), check_vma=False
    )
```

```python
import functools

import jax
import jax.numpy as jnp
from jax import lax
from jax.experimental import pallas as pl
from jax.experimental.pallas import tpu as pltpu
from jax.sharding import PartitionSpec as P


LANES = 128
VMEM_LIMIT = 16 * 1024 * 1024


def split(value):
    high = value.astype(jnp.bfloat16)
    return high, (value - high.astype(jnp.float32)).astype(jnp.bfloat16)


def product(left_high, left_low, right_high, right_low):
    dot = functools.partial(jnp.dot, preferred_element_type=jnp.float32)
    return dot(left_high, right_high) + (dot(left_high, right_low) + dot(left_low, right_high))


def fetch(slot, flag, first, buffer, sem):
    count = buffer.shape[0]
    copies = []
    for ref, skip in zip(slot, first):
        copies.append(pltpu.make_async_copy(ref.at[pl.ds(skip, count)], buffer, sem))
    if len(copies) == 1:
        copies[0].start()
    else:
        pl.when(flag != 0)(copies[0].start)
        pl.when(flag == 0)(copies[1].start)
    return copies[0]


def add_kernel(counts, pieces, keep, scalars, acc_ref, *refs):
    right, refs = refs[:pieces], refs[pieces:]
    slots = []
    for count in counts:
        slots.append(refs[:count])
        refs = refs[count:]
    out_ref, right_high, right_low, buffers, sems, turned, left_high, left_low = refs
    width, rows = slots[0][0].shape[1:]
    row_blocks = buffers.shape[1]
    cut = right[0].shape[1]
    step = pl.program_id(0)
    lanes = pl.ds(pl.multiple_of(step * cut, cut), cut)
    mine = lanes if keep else slice(None)

    def copies(start):
        for index, slot in enumerate(slots):
            if start:
                fetch(slot, scalars[2 * index + 1], (0, 0), buffers.at[index], sems.at[index])
            else:
                pltpu.make_async_copy(slot[0].at[pl.ds(0, row_blocks)], buffers.at[index], sems.at[index]).wait()

    @pl.when(step == 0)
    def _():
        copies(True)
        turned[...] = jnp.zeros_like(turned)

    at = 0
    for piece in right:
        high, low = split(piece[...])
        right_high[at : at + piece.shape[0], mine] = high
        right_low[at : at + piece.shape[0], mine] = low
        at += piece.shape[0]

    @pl.when(step == 0)
    def _():
        copies(False)

        def one(block, carry):
            for index in range(len(slots)):
                at = pl.multiple_of(scalars[2 * index] * width, width)
                turned[pl.ds(at, width), :] = buffers[index, block]
            high, low = split(turned[...].T)
            at = pl.multiple_of(block * rows, rows)
            left_high[pl.ds(at, rows), :] = high
            left_low[pl.ds(at, rows), :] = low
            return carry

        lax.fori_loop(0, row_blocks, one, 0)

    out_ref[:, lanes] = acc_ref[:, lanes] - product(
        left_high[...], left_low[...], right_high[:, mine], right_low[:, mine]
    )


def add(acc, slots, scalars, right, keep):
    rows, cols = acc.shape
    depth = sum(piece.shape[0] for piece in right)
    flat = [array for slot in slots for array in slot]
    cut = min(cols, 2 * LANES)
    resident = pl.BlockSpec(memory_space=pltpu.VMEM)
    used = len(slots) * flat[0].shape[1]
    shape = jax.ShapeDtypeStruct((depth, cols), jnp.bfloat16)
    terms = [pltpu.VMEM((depth, cut), jnp.bfloat16)] * 2
    return pl.pallas_call(
        functools.partial(add_kernel, [len(slot) for slot in slots], len(right), keep),
        out_shape=[jax.ShapeDtypeStruct(acc.shape, acc.dtype)] + [shape, shape] * keep,
        grid_spec=pltpu.PrefetchScalarGridSpec(
            num_scalar_prefetch=1,
            grid=(cols // cut,),
            in_specs=[resident]
            + [pl.BlockSpec((piece.shape[0], cut), lambda i, s: (0, i)) for piece in right]
            + [pl.BlockSpec(memory_space=pl.ANY)] * len(flat),
            out_specs=[resident] + [resident] * (2 * keep),
            scratch_shapes=terms * (not keep)
            + [
                pltpu.VMEM((len(slots),) + flat[0].shape, jnp.float32),
                pltpu.SemaphoreType.DMA((len(slots),)),
                pltpu.VMEM((depth, flat[0].shape[2]), jnp.float32),
                pltpu.VMEM((rows, depth), jnp.bfloat16),
                pltpu.VMEM((rows, depth), jnp.bfloat16),
            ],
        ),
        input_output_aliases={1: 0},
        compiler_params=pltpu.CompilerParams(vmem_limit_bytes=VMEM_LIMIT),
        cost_estimate=pl.CostEstimate(
            flops=6 * rows * used * cols, bytes_accessed=4 * depth * cols, transcendentals=0
        ),
        name="add",
    )(scalars, acc, *right, *flat)


def fold_kernel(blocks, x_ref, acc_ref):
    rows = x_ref.shape[0] // blocks
    mine = pl.ds(pl.multiple_of(pl.program_id(0) * rows, rows), rows)
    for block in range(blocks):
        acc_ref[mine, block * LANES : (block + 1) * LANES] = x_ref[pl.ds(block, rows, stride=blocks), :]


def fold(front):
    row_blocks, height, blocks, lanes = front.shape
    rows, cols = row_blocks * height, blocks * lanes
    return pl.pallas_call(
        functools.partial(fold_kernel, blocks),
        out_shape=jax.ShapeDtypeStruct((rows, cols), front.dtype),
        grid=(row_blocks,),
        in_specs=[pl.BlockSpec((height * blocks, lanes), lambda i: (i, 0))],
        out_specs=pl.BlockSpec(memory_space=pltpu.VMEM),
        compiler_params=pltpu.CompilerParams(vmem_limit_bytes=VMEM_LIMIT),
        cost_estimate=pl.CostEstimate(flops=0, bytes_accessed=4 * front.size, transcendentals=0),
        name="fold",
    )(front.reshape(rows * blocks, lanes))


def one_kernel(count, scalars, acc_ref, high_ref, low_ref, *refs):
    slot = refs[:count]
    out_ref, buffer, sem, left = refs[count:]
    row_blocks, width, height = buffer.shape
    cut = acc_ref.shape[1] // pl.num_programs(0)
    step = pl.program_id(0)

    @pl.when(step == 0)
    def _():
        fetch(slot, scalars[1], (0, 0), buffer, sem).wait()
        for block in range(row_blocks):
            high, low = split(buffer[block].T)
            left[block * height : (block + 1) * height, :] = high
            low_row = (row_blocks + block) * height
            left[low_row : low_row + height, :] = low

    pivots = pl.ds(pl.multiple_of(scalars[0] * width, width), width)
    lanes = pl.ds(pl.multiple_of(step * cut, cut), cut)
    rows = acc_ref.shape[0]
    both = jnp.dot(left[...], high_ref[pivots, lanes], preferred_element_type=jnp.float32)
    rest = jnp.dot(left[:rows, :], low_ref[pivots, lanes], preferred_element_type=jnp.float32)
    out_ref[:, lanes] = acc_ref[:, lanes] - (both[:rows] + (both[rows:] + rest))


def one(acc, slot, scalars, right):
    rows, cols = acc.shape
    width = slot[0].shape[1]
    cut = min(cols, 2 * LANES)
    resident = pl.BlockSpec(memory_space=pltpu.VMEM)
    return pl.pallas_call(
        functools.partial(one_kernel, len(slot)),
        out_shape=jax.ShapeDtypeStruct(acc.shape, acc.dtype),
        grid_spec=pltpu.PrefetchScalarGridSpec(
            num_scalar_prefetch=1,
            grid=(cols // cut,),
            in_specs=[resident] * 3 + [pl.BlockSpec(memory_space=pl.ANY)] * len(slot),
            out_specs=resident,
            scratch_shapes=[
                pltpu.VMEM(slot[0].shape, jnp.float32),
                pltpu.SemaphoreType.DMA,
                pltpu.VMEM((2 * rows, width), jnp.bfloat16),
            ],
        ),
        input_output_aliases={1: 0},
        compiler_params=pltpu.CompilerParams(vmem_limit_bytes=VMEM_LIMIT),
        cost_estimate=pl.CostEstimate(flops=6 * rows * width * cols, bytes_accessed=4 * slot[0].size, transcendentals=0),
        name="one",
    )(scalars, acc, right[0], right[1], *slot)


def last_kernel(blocks, count, first, base, scalars, acc_ref, high_ref, low_ref, *refs):
    slot = refs[:count]
    out_ref, _, buffer, sem = refs[-4:]
    _, width, height = buffer.shape
    rows = out_ref.shape[0] // blocks
    row_blocks = rows // height
    step = pl.program_id(0)

    @pl.when(step == 0)
    def _():
        fetch(slot, scalars[1], first, buffer, sem).wait()

    parts = [split(buffer[step * row_blocks + block].T) for block in range(row_blocks)]
    left_high = jnp.concatenate([part[0] for part in parts], axis=0)
    left_low = jnp.concatenate([part[1] for part in parts], axis=0)
    left_both = jnp.concatenate([left_high, left_low], axis=0)
    pivots = pl.ds(pl.multiple_of(scalars[0] * width, width), width)
    mine = pl.ds(pl.multiple_of(base + step * rows, rows), rows)
    pair = min(blocks, 2)
    for block in range(0, blocks, pair):
        lanes = pl.ds(block * LANES, pair * LANES)
        both = jnp.dot(left_both, high_ref[pivots, lanes], preferred_element_type=jnp.float32)
        rest = jnp.dot(left_high, low_ref[pivots, lanes], preferred_element_type=jnp.float32)
        value = acc_ref[mine, lanes] - (both[:rows] + (both[rows:] + rest))
        for one in range(pair):
            out_ref[pl.ds(block + one, rows, stride=blocks), :] = value[:, one * LANES : (one + 1) * LANES]


def last(acc, slot, first, scalars, right, blocks, first_block, row_blocks, buffer):
    rows, cols = acc.shape
    width, height = slot[0].shape[1:]
    step = 2 if row_blocks % 4 == 0 else 1
    base = first_block // step
    buffers = () if buffer is None else (buffer,)
    resident = pl.BlockSpec(memory_space=pltpu.VMEM)
    return pl.pallas_call(
        functools.partial(last_kernel, blocks, len(slot), first, first_block * height),
        out_shape=[
            jax.ShapeDtypeStruct((rows * blocks, LANES), acc.dtype),
            jax.ShapeDtypeStruct(acc.shape, acc.dtype),
        ],
        grid_spec=pltpu.PrefetchScalarGridSpec(
            num_scalar_prefetch=1,
            grid=(row_blocks // step,),
            in_specs=[resident] * 3 + [pl.BlockSpec(memory_space=pl.ANY)] * (len(slot) + len(buffers)),
            out_specs=[pl.BlockSpec((step * height * blocks, LANES), lambda i, s: (base + i, 0)), resident],
            scratch_shapes=[
                pltpu.VMEM((row_blocks, width, height), jnp.float32),
                pltpu.SemaphoreType.DMA,
            ],
        ),
        input_output_aliases={1: 1, 4 + len(slot): 0} if buffers else {1: 1},
        compiler_params=pltpu.CompilerParams(vmem_limit_bytes=VMEM_LIMIT),
        cost_estimate=pl.CostEstimate(
            flops=6 * row_blocks * height * width * cols, bytes_accessed=4 * row_blocks * height * cols, transcendentals=0
        ),
        name="last",
    )(scalars, acc, right[0], right[1], *slot, *buffers)


def moves(count):
    power = count & (count - 1) == 0
    pairs = lambda m: [(i, i ^ m if power else (i + m) % count) for i in range(count)]
    source = lambda me, m: me ^ m if power else lax.rem(me + count - m, count)
    target = lambda me, m: me ^ m if power else lax.rem(me + m, count)
    return power, pairs, source, target


def line(piece, axis, count, tails):
    mate = lambda i, odd: i + 1 if i % 2 == odd else i - 1
    reach = lambda i, odd: count - 1 - i if i % 2 == odd else i
    streams = {0: [], 1: []}
    for step in range(1, count):
        new = {}
        for odd in (0, 1):
            pairs = [(mate(i, odd), i) for i in range(count) if reach(i, odd) >= step]
            if pairs:
                what = piece if step == 1 else streams[1 - odd][step - 2]
                if len(tails) > 1 and odd == 0 and step == count - 1:
                    parts = [what[sum(tails[:n]) : sum(tails[: n + 1])] for n in range(len(tails))]
                    new[odd] = [lax.ppermute(part, axis, pairs) for part in parts]
                else:
                    new[odd] = lax.ppermute(what, axis, pairs)
        for odd, value in new.items():
            streams[odd].append(value)
    return streams


def local(sizes, contribution, left_panel, right_panel):
    n_row, n_col, n_kk = sizes["row"], sizes["col"], sizes["kk"]
    row, col, kk = lax.axis_index("row"), lax.axis_index("col"), lax.axis_index("kk")
    row_blocks, height, blocks, lanes = contribution.shape
    cols = blocks * lanes
    width = left_panel.shape[3]
    depth = right_panel.shape[1]
    quarter = depth * n_row
    order = sorted(range(n_kk), key=lambda m: (bin(m).count("1"), m))

    power, pairs, _, target = moves(n_kk)
    left = left_panel.transpose(0, 2, 3, 1).reshape(n_kk, row_blocks, width, height)
    group = lambda index: lax.dynamic_index_in_dim(left, index, 0, keepdims=False)
    groups = [group(kk)] + [group(target(kk, m)) for m in order[1:2]]
    *groups, left = lax.optimization_barrier((*groups, left))
    groups += [group(target(kk, m)) for m in order[2:]]
    pieces = [groups[0] if m == 0 else lax.ppermute(groups[i], "kk", pairs(m)) for i, m in enumerate(order)]

    tails = [(row_blocks + 2 - n) // 3 for n in range(3)] if row_blocks > 2 and n_col > 2 else [row_blocks]
    streams = [line(piece, "col", n_col, tails if i == n_kk - 1 else ()) for i, piece in enumerate(pieces)]
    even = col % 2 == 0
    length = jnp.where(even, n_col - 1 - col, col)
    lengths = sorted({n_col - 1 - i if i % 2 == 0 else i for i in range(n_col)})

    def slot_of(piece, stream, index):
        if index == 0:
            return (piece,)
        near, far = stream[0], stream[1]
        options = [(reach, far[index - 1 - reach]) for reach in lengths if index > reach]
        if not options:
            return (near[index - 1],)
        value = options[-1][1]
        for reach, other in options[:-1]:
            value = jnp.where(length == reach, other, value)
        return (near[index - 1], value) if index <= lengths[-1] else (value,)

    def scalars_of(index):
        if index == 0:
            return [col, jnp.int32(1)]
        past = index - length
        by_near = jnp.where(even, col + index, col - index)
        by_far = jnp.where(even, col - past, col + past)
        is_near = index <= length
        return [jnp.where(is_near, by_near, by_far), is_near.astype(jnp.int32)]

    own = right_panel.reshape(depth, cols)
    parts = {0: [own]}
    for m in order:
        bits = [1 << b for b in range(n_kk.bit_length()) if m >> b & 1]
        if m == 0:
            continue
        if not power or len(bits) == 1:
            parts[m] = [lax.ppermute(own, "kk", pairs(m))]
        else:
            half = depth // 2
            whole = lambda piece: piece[0] if len(piece) == 1 else jnp.concatenate(piece, axis=0)
            first = lax.ppermute(whole(parts[m ^ bits[0]])[:half], "kk", pairs(bits[0]))
            second = lax.ppermute(whole(parts[m ^ bits[-1]])[half:], "kk", pairs(bits[-1]))
            parts[m] = [first, second]

    row_power, row_pairs, row_source, _ = moves(n_row)
    rights = []
    for i, m in enumerate(order):
        rights.append(list(parts[m]))
        for j in range(1, n_row):
            rights[i] += [lax.ppermute(part, "row", row_pairs(j)) for part in parts[m]]
    if depth % width == 0:
        per = depth // width

        def place(shard):
            rank = shard // per
            return (rank ^ row if row_power else lax.rem(row - rank + n_row, n_row)) * per + lax.rem(shard, per)

    else:
        place = lambda shard: shard
        for i, right in enumerate(rights):
            count = len(right) // n_row
            total = jnp.zeros((quarter, cols), jnp.float32)
            for j in range(n_row):
                piece = jnp.concatenate(right[j * count : (j + 1) * count], axis=0)
                rank = row if j == 0 else row_source(row, j)
                total = lax.dynamic_update_slice_in_dim(total, piece, rank * depth, 0)
            rights[i] = [total]

    scalars = []
    for index in range(n_col):
        shard, flag = scalars_of(index)
        scalars += [place(shard), flag]
    scalars = jnp.stack(scalars).astype(jnp.int32)

    acc = fold(contribution)
    final = n_kk - 1
    early = max(n_col - 2, 1)
    for i in [*range(final - 1), final, final - 1]:
        slots = [slot_of(pieces[i], streams[i], index) for index in range(early if i == final else n_col)]
        acc, *terms = add(acc, slots, scalars, rights[i], i == final)
        if terms:
            kept = terms
    for index in range(early, n_col - 1):
        slot = slot_of(pieces[final], streams[final], index)
        acc = one(acc, slot, scalars[2 * index : 2 * index + 2], kept)

    out, start = None, 0
    for part, count in enumerate(tails):
        stream = {0: list(streams[final][0]), 1: streams[final][1]}
        if len(tails) > 1:
            stream[0][-1] = stream[0][-1][part]
        options = slot_of(pieces[final], stream, n_col - 1)
        first = [0 if option.shape[0] == count else start for option in options]
        out, acc = last(acc, options, first, scalars[-2:], kept, blocks, start, count, out)
        start += count
    return out.reshape(contribution.shape)


def solution(mesh):
    placed = (P("kk", "row", None, "col"), P(None, "row", "kk", "col"), P("kk", "row", None, "col"))

    def body(*args):
        return local(dict(mesh.shape), *args)

    return jax.shard_map(
        body, mesh=mesh, in_specs=placed, out_specs=P("kk", "row", None, "col"), check_vma=False
    )
```
